32 devices in a mesh: member: 2 (over core), shard: 16 (over z, y, x).
Axes of the slice: x: 2, y: 2, z: 4, core: 2. Of those that a mesh axis runs over, the one named last changes fastest.
Arguments:
- layer_input: bfloat16 [2, 180, 5120], P('member', None, 'shard'), may hold values from -6 to 6
- norm_gain: float32 [2, 5120], P('member'), may hold values from 0.5 to 2
- w_gate: bfloat16 [2, 5120, 1792], P('member', None, 'shard'), may hold values from -0.0559017 to 0.0559017
- w_up: bfloat16 [2, 5120, 1792], P('member', None, 'shard'), may hold values from -0.0559017 to 0.0559017
- hidden_cot: bfloat16 [2, 180, 1792], P('member', None, 'shard'), may hold values from -3 to 5
- output_cot: bfloat16 [2, 180, 5120], P('member', None, 'shard'), may hold values from -6 to 6
- embed: bfloat16 [2, 4096, 5120], P('member', 'shard'), may hold values from -0.078125 to 0.078125
- suffix_ids: int32 [180], replicated, may hold values from 0 to 4095
Outputs:
- delta: float32 [180, 4096], P(None, 'shard')
The draws below stay inside these ranges and needn't reach their ends.
All inputs are finite; a program needn't handle non-finite values.
Results may differ from the reference program's by a relative error of at most 0.0047.
Values may be sent and summed in bfloat16 or wider, within the bound.
A program may use at most 64 MiB of HBM per device.

```python
import math
import jax
import jax.numpy as jnp
from jax import lax

D = 5120
MEMBERS = 2
FFW = 1792
VOCAB = 4096
ROWS = 180


def weight_draw(key, own_tag):
    shape = (MEMBERS, D, FFW)
    common_part = jax.random.normal(jax.random.fold_in(key, 101), shape, jnp.float32)
    own_part = jax.random.normal(jax.random.fold_in(key, own_tag), shape, jnp.float32)
    mixed = 0.9 * common_part + 0.43588989 * own_part
    mixed = jnp.clip(mixed, -3.98, 3.98)
    return (mixed / jnp.sqrt(jnp.float32(D))).astype(jnp.bfloat16)


def draw_w_gate(key, part):
    return weight_draw(key, 102)


def draw_w_up(key, part):
    return weight_draw(key, 103)


def draw_hidden_cot(key, part):
    shape = (MEMBERS, ROWS, FFW)
    row_mean = jnp.ones((MEMBERS, ROWS, 1), jnp.float32)
    noise = jax.random.normal(jax.random.fold_in(key, 202), shape, jnp.float32)
    values = jnp.clip(row_mean + noise, -3.0, 5.0)
    return values.astype(jnp.bfloat16)


def place_ends(array, stream_key, least, top_value):
    longest = array.shape.index(max(array.shape))
    spots = []
    for shift in (0, 1):
        where = [jax.random.randint(jax.random.fold_in(stream_key, axis), (), 0, length) for axis, length in enumerate(array.shape)]
        where[longest] = (where[longest] + shift) % array.shape[longest]
        spots.append(tuple(where))
    return array.at[spots[0]].set(least).at[spots[1]].set(top_value)


def block_scale(own_key, extent, shards, least, largest):
    level, own = 1.0, jax.random.fold_in(own_key, 6)
    for dim, blocks in shards:
        draws = jnp.exp(jax.random.uniform(jax.random.fold_in(own, dim), (blocks,), jnp.float32, least / len(shards), largest / len(shards)))
        level = level * jnp.repeat(draws, extent[dim] // blocks).reshape([-1 if axis == dim else 1 for axis in range(len(extent))])
    return level


def scatter_about(key, dims, deviation, limit, shards=(), dtype=jnp.bfloat16):
    result = jax.random.normal(key, dims, jnp.float32) * deviation
    if len(shards) > 0:
        result = block_scale(key, dims, shards, -0.22, 0.18) * result
    return jnp.clip(result, min=-limit, max=limit).astype(dtype)


def setup_inputs(seed: int = 0) -> dict:
    key_list = jax.random.split(jax.random.key(seed), 9)
    return {
        "layer_input": scatter_about(key_list[0], (MEMBERS, ROWS, D), 1.0, 6.0, ((0, 2), (2, 16))),
        "norm_gain": jnp.clip(jnp.exp(math.log(2.0) - 1.3862944 * jax.random.uniform(key_list[1], (MEMBERS, D), jnp.float32) ** block_scale(key_list[1], (MEMBERS, D), ((0, 2),), -0.2, 0.2)), 0.5, 2.0),
        "w_gate": draw_w_gate(jax.random.fold_in(key_list[8], 71), 0),
        "w_up": draw_w_up(jax.random.fold_in(key_list[8], 71), 0),
        "hidden_cot": draw_hidden_cot(jax.random.fold_in(key_list[8], 71), 0),
        "output_cot": scatter_about(key_list[5], (MEMBERS, ROWS, D), 1.0, 6.0, ((0, 2), (2, 16))),
        "embed": scatter_about(key_list[6], (MEMBERS, VOCAB, D), D ** -0.5, 0.078125, ((0, 2), (1, 16))),
        "suffix_ids": place_ends(jax.random.randint(key_list[7], (ROWS,), 0, VOCAB), jax.random.fold_in(key_list[7], 1), 0, VOCAB - 1).astype(jnp.int32),
    }


def member_term(inputs_bf, gain, gate_w, up_w, hid_grad, out_grad, table, suffix_ids):
    inputs = inputs_bf.astype(jnp.float32)
    inv_rms = 1.0 / jnp.sqrt(lax.optimization_barrier(jnp.mean(inputs * inputs, axis=1, keepdims=True)) + 1e-05)
    normed = (inputs * inv_rms * gain[None, :]).astype(jnp.bfloat16)
    gate_pre = jnp.dot(normed, gate_w, preferred_element_type=jnp.float32)
    up_proj = jnp.dot(normed, up_w, preferred_element_type=jnp.float32)
    sigmoid_gate = jax.nn.sigmoid(gate_pre)
    hid_f = hid_grad.astype(jnp.float32)
    gate_grad = (hid_f * up_proj * sigmoid_gate * (1.0 + gate_pre * (1.0 - sigmoid_gate))).astype(jnp.bfloat16)
    up_grad = (hid_f * gate_pre * sigmoid_gate).astype(jnp.bfloat16)
    normed_grad = jnp.dot(gate_grad, gate_w.T, preferred_element_type=jnp.float32)
    normed_grad = normed_grad + jnp.dot(up_grad, up_w.T, preferred_element_type=jnp.float32)
    scaled = normed_grad * gain[None, :]
    proj = lax.optimization_barrier(jnp.mean(inputs * scaled, axis=1, keepdims=True))
    input_grad = out_grad.astype(jnp.float32) + inv_rms * scaled - inputs * inv_rms ** 3 * proj
    input_grad = input_grad.astype(jnp.bfloat16)
    scores = jnp.dot(input_grad, table.T, preferred_element_type=jnp.float32)
    current = jnp.take_along_axis(scores, suffix_ids[:, None].astype(jnp.int32), axis=1)
    return scores - current

def reference(layer_input, norm_gain, w_gate, w_up, hidden_cot, output_cot, embed, suffix_ids):
    total = jnp.zeros((ROWS, VOCAB), jnp.float32)
    for member in range(MEMBERS):
        total = total + member_term(layer_input[member], norm_gain[member], w_gate[member], w_up[member], hidden_cot[member], output_cot[member], embed[member], suffix_ids)
    return total
```

```python
import functools

import jax
import jax.numpy as jnp
from jax import lax
from jax.experimental import pallas as pl
from jax.experimental.pallas import tpu as pltpu
from jax.sharding import PartitionSpec as P

F32 = jnp.float32
BF16 = jnp.bfloat16
NT = (((1,), (1,)), ((), ()))
TN = (((0,), (0,)), ((), ()))
HIGH = lax.Precision.HIGHEST
LAG = 0
PARTS = 1


def grid_of(n):
    inner = 1
    while (2 * inner) ** 3 <= n:
        inner *= 2
    return n // (inner * inner), inner, inner


def ceil_to(v, m):
    return -(-v // m) * m


def fold_of(rp):
    return ceil_to(rp, 16) // 2


def packed_rows(rp, dl):
    q, r = divmod(dl, 128)
    return q * rp + (0 if r == 0 else fold_of(rp) if r <= 64 else rp)


def pack(value):
    rp, dl = value.shape
    q, r = divmod(dl, 128)
    pieces = [value[:, k * 128:(k + 1) * 128] for k in range(q)]
    if r:
        tail = value[:, q * 128:]
        if r <= 64:
            fold = fold_of(rp)
            tail = jnp.concatenate([tail, jnp.zeros((rp, 64 - r), tail.dtype)], axis=1) if r < 64 else tail
            upper = tail[fold:]
            if rp < 2 * fold:
                upper = jnp.concatenate([upper, jnp.zeros((2 * fold - rp, 64), tail.dtype)], axis=0)
            tail = jnp.concatenate([tail[:fold], upper], axis=1)
        else:
            tail = jnp.concatenate([tail, jnp.zeros((rp, 128 - r), tail.dtype)], axis=1)
        pieces.append(tail)
    return jnp.concatenate(pieces, axis=0) if len(pieces) > 1 else pieces[0]


def unpack(packed, rp, dl):
    q, r = divmod(dl, 128)
    pieces = [packed[k * rp:(k + 1) * rp] for k in range(q)]
    if r:
        tail = packed[q * rp:]
        if r <= 64:
            fold = fold_of(rp)
            tail = jnp.concatenate([tail[:, :r], tail[:rp - fold, 64:64 + r]], axis=0)
        else:
            tail = tail[:, :r]
        pieces.append(tail)
    return jnp.concatenate(pieces, axis=1) if len(pieces) > 1 else pieces[0]


def gather_sends(lines):
    A, B, C = lines
    line, diag = B + C - 2, (B - 1) * (C - 1)
    return (A - 1) + 2 * line + 2 * diag + line + (A - 2) * 2 * line + diag + (A - 2) * 2 * diag


CHUNK_BUFFERS = (
    "xg", "gg", "part", "rx", "ry", "rz", "rd", "r1y", "r1x", "st_in", "st_pr", "st_cu",
    "acc", "hcat", "inv", "ssq", "scores", "others", "total",
    "x_send", "x_recv", "g_send", "g_recv", "p_send", "qx", "qy", "qz", "qd", "q1y", "q1x",
    "st_send", "st_recv", "m_send", "m_recv",
)
SHARED = ("wg_v", "wu_v", "wt3", "emb_v", "emb3", "gain3", "idcol", "load_sem")


def kernel(n, members, lines, chunks, width, x_in, gain_in, hid_in, cot_in, ids_in, wg_hbm, wu_hbm, emb_hbm,
           out_ref, *scratch):
    A, B, C = lines
    dl = x_in.shape[1]
    fl = hid_in.shape[1]
    vl = emb_hbm.shape[0]
    rows = x_in.shape[0]
    S = dict(zip(SHARED, scratch))
    scratch = scratch[len(SHARED):]
    K = [dict(zip(CHUNK_BUFFERS, scratch[k * len(CHUNK_BUFFERS):])) for k in range(len(chunks))]
    wt3, emb3, gain3, idcol = S["wt3"], S["emb3"], S["gain3"], S["idcol"]
    flp = wt3.shape[1] // 2
    me = lax.axis_index("shard")
    mine = lax.axis_index("member")
    c0 = lax.rem(me, C)
    b0 = lax.rem(lax.div(me, C), B)
    a0 = lax.div(me, B * C)

    def at(a, b, c):
        return (a * B + b) * C + c

    def turn(v, d, size):
        if size & (size - 1):
            return lax.rem(v + d, size)
        for k in range(size.bit_length() - 1):
            bit = 2 ** k
            on = (d // bit) % 2 if isinstance(d, int) else lax.rem(lax.div(d, bit), 2)
            v = v + on * (bit - 2 * bit * lax.rem(lax.div(v, bit), 2))
        return v

    def remote(src, dst, send, recv, peer, axis="shard"):
        return pltpu.make_async_remote_copy(
            src_ref=src, dst_ref=dst, send_sem=send, recv_sem=recv,
            device_id={axis: peer}, device_id_type=pl.DeviceIdType.MESH,
        )

    plane = [turn(a0, d, A) for d in range(A)]
    xs = [turn(c0, d, C) for d in range(1, C)]
    ys = [turn(b0, d, B) for d in range(1, B)]

    loads = [
        pltpu.make_async_copy(wg_hbm, S["wg_v"], S["load_sem"].at[0]),
        pltpu.make_async_copy(wu_hbm, S["wu_v"], S["load_sem"].at[1]),
        pltpu.make_async_copy(emb_hbm, S["emb_v"], S["load_sem"].at[2]),
    ]
    for load in loads:
        load.start()

    barrier = pltpu.get_barrier_semaphore()
    for d in range(1, n):
        pl.semaphore_signal(barrier, inc=1, device_id={"shard": turn(me, d, n)},
                            device_id_type=pl.DeviceIdType.MESH)
    for d in range(1, members):
        pl.semaphore_signal(barrier, inc=1, device_id={"member": turn(mine, d, members)},
                            device_id_type=pl.DeviceIdType.MESH)

    def first_row(k):
        return (lax.broadcasted_iota(jnp.int32, (8, k), 0) == 0).astype(F32)

    def to_row(values):
        return lax.dot_general(first_row(values.shape[1]), values, NT, precision=HIGH,
                               preferred_element_type=F32)[0:1]

    def to_column(row, lanes):
        rows8 = first_row(row.shape[1]) * row
        return lax.dot_general(rows8, jnp.ones((8, lanes), F32), TN, precision=HIGH,
                               preferred_element_type=F32)

    def pad_rows(value, rp):
        short = rp - value.shape[0]
        return jnp.concatenate([value, jnp.zeros((short, value.shape[1]), value.dtype)], axis=0) if short else value

    waits = []

    def start(copies):
        waits.extend(copies)
        for copy in copies:
            copy.start()

    def halves_of(length):
        low = ceil_to(length // 2, 8)
        return pl.ds(0, low), pl.ds(low, length - low)

    def gather(buf, send, recv, process):
        spans = halves_of(buf.shape[1])
        used = [0]

        def move(blk, h, peer, slot):
            view = buf.at[blk] if h is None else buf.at[blk, spans[h]]
            return remote(view, view, send.at[slot], recv.at[blk, h or 0], peer)

        def piece(blk, h, peer):
            used[0] += 1
            return move(blk, h, peer, used[0] - 1)

        def arrive(blk, h, peer):
            move(blk, h, peer, 0).wait_recv()

        def spread(j):
            blk = at(plane[j], b0, c0)
            if j == 1:
                return [piece(blk, None, at(a0, b0, c)) for c in xs] + [piece(blk, None, at(a0, b, c0)) for b in ys]
            copies = []
            for h in (0, 1):
                copies += [piece(blk, h, at(a0, b0, c)) for c in xs]
                copies += [piece(blk, 1 - h, at(a0, b, c0)) for b in ys]
            return copies

        def cross(j):
            for c in xs:
                arrive(at(plane[j], b0, c), 0, at(a0, b0, c))
                start([piece(at(plane[j], b0, c), 0, at(a0, b, c0)) for b in ys])
            for b in ys:
                arrive(at(plane[j], b, c0), 1, at(a0, b, c0))
                start([piece(at(plane[j], b, c0), 1, at(a0, b0, c)) for c in xs])

        def rest(j):
            for c in xs:
                arrive(at(plane[j], b0, c), 1, at(a0, b0, c))
            for b in ys:
                arrive(at(plane[j], b, c0), 0, at(a0, b, c0))

        def sides(j):
            return [at(plane[j], b0, c) for c in xs] + [at(plane[j], b, c0) for b in ys]

        cells = [(b, c) for b in ys for c in xs]

        def level0():
            start([piece(me, None, at(plane[j], b0, c0)) for j in range(1, A)])
            start(spread(0))

        def level1():
            process([me])
            cross(0)
            for j in range(1, A):
                arrive(at(plane[j], b0, c0), None, at(plane[j], b0, c0))
                start(spread(j))
            rest(0)
            process(sides(0))
            process([at(plane[j], b0, c0) for j in range(1, A)])

        def level2():
            for b, c in cells:
                arrive(at(a0, b, c), 0, at(a0, b, c0))
                arrive(at(a0, b, c), 1, at(a0, b0, c))
                start([piece(at(a0, b, c), None, at(plane[1], b0, c0))])
            for j in range(2, A):
                cross(j)
            process([at(a0, b, c) for b, c in cells])
            for c in xs:
                arrive(at(plane[1], b0, c), None, at(a0, b0, c))
            for b in ys:
                arrive(at(plane[1], b, c0), None, at(a0, b, c0))
            process(sides(1))
            for j in range(2, A):
                rest(j)
                process(sides(j))

        def level3():
            for j in range(2, A):
                for b, c in cells:
                    arrive(at(plane[j], b, c), 0, at(a0, b, c0))
                    arrive(at(plane[j], b, c), 1, at(a0, b0, c))
                process([at(plane[j], b, c) for b, c in cells])
            for b, c in cells:
                arrive(at(plane[1], b, c), None, at(plane[1], b0, c0))
            process([at(plane[1], b, c) for b, c in cells])

        return [level0, level1, level2, level3]

    def program(k):
        r0, real, rp = chunks[k]
        T = K[k]
        length = T["xg"].shape[1]
        lo, hi = halves_of(length)
        part, rx, ry, rz, rd = T["part"], T["rx"], T["ry"], T["rz"], T["rd"]
        st_in, st_send, st_recv = T["st_in"], T["st_send"], T["st_recv"]

        def own_x():
            return pad_rows(x_in[r0:r0 + real].astype(F32), rp)

        def stat_copy(i, buf, d):
            return remote(st_in.at[i], buf.at[me], st_send.at[i, d], st_recv.at[i, me], turn(me, d, n))

        def stat_send(i, buf):
            start([stat_copy(i, buf, d) for d in range(1, n)])

        def stat_sum(i, buf):
            sum_ = st_in[i]
            for d in range(1, n):
                src = turn(me, d, n)
                remote(st_in.at[i], buf.at[src], st_send.at[i, d], st_recv.at[i, src], src).wait_recv()
                sum_ = sum_ + buf[src]
            return sum_

        def up(blocks):
            for blk in blocks:
                raw = T["xg"][blk].astype(F32)
                T["ssq"][...] += raw * raw
                scaled = (unpack(raw, rp, dl) * gain3[blk]).astype(BF16)
                T["acc"][...] += lax.dot_general(scaled, wt3[blk], NT, preferred_element_type=F32)

        def activate():
            square = jnp.sum(unpack(T["ssq"][...], rp, dl), axis=1, keepdims=True)
            inv = 1.0 / jnp.sqrt(square / width + 1e-05)
            T["inv"][...] = jnp.broadcast_to(inv, (rp, 128))
            gate_pre = T["acc"][:, 0:flp] * inv
            up_proj = T["acc"][:, flp:2 * flp] * inv
            hid = pad_rows(hid_in[r0:r0 + real].astype(F32), rp)
            if flp > fl:
                hid = jnp.concatenate([hid, jnp.zeros((rp, flp - fl), F32)], axis=1)
            s = jax.nn.sigmoid(gate_pre)
            gate_grad = (hid * up_proj * s * (1.0 + gate_pre * (1.0 - s))).astype(BF16)
            up_grad = (hid * gate_pre * s).astype(BF16)
            T["hcat"][:, 0:flp] = gate_grad
            T["hcat"][:, flp:2 * flp] = up_grad
            st_in[0] = to_row(gate_grad.astype(F32) * gate_pre + up_grad.astype(F32) * up_proj)
            stat_send(0, T["st_pr"])

        def product(blk):
            return pack(jnp.dot(T["hcat"][...], wt3[blk], preferred_element_type=F32))

        def landed(slot, sem, peer):
            remote(slot, slot, T["p_send"].at[0, 0], sem, peer).wait_recv()
            return slot[...].astype(F32)

        def out(blk, h, span, dst, sem, peer):
            view = part.at[blk] if span is None else part.at[blk, span]
            return remote(view, dst, T["p_send"].at[blk, h], sem, peer)

        cells = [(b, c) for b in ys for c in xs]

        def split(blk, j, b, c):
            start([
                out(blk, 0, lo, T["r1y"].at[plane[j], c, b0, lo], T["q1y"].at[plane[j], c, b0], at(a0, b, c0)),
                out(blk, 1, hi, T["r1x"].at[plane[j], b, c0, hi], T["q1x"].at[plane[j], b, c0], at(a0, b0, c)),
            ])

        def side_sums(j):
            for c in xs:
                blk = at(plane[j], b0, c)
                value = product(blk)
                if j == 1:
                    part[blk] = value.astype(BF16)
                else:
                    edge = value[:lo.size]
                    for b in ys:
                        edge = edge + landed(T["r1y"].at[plane[j], c, b, lo], T["q1y"].at[plane[j], c, b], at(a0, b, c0))
                    part[blk, lo] = edge.astype(BF16)
                    part[blk, hi] = value[lo.size:].astype(BF16)
                start([out(blk, 0, None, rx.at[plane[j], c0], T["qx"].at[plane[j], c0], at(a0, b0, c))])
            for b in ys:
                blk = at(plane[j], b, c0)
                value = product(blk)
                if j == 1:
                    part[blk] = value.astype(BF16)
                else:
                    edge = value[lo.size:]
                    for c in xs:
                        edge = edge + landed(T["r1x"].at[plane[j], b, c, hi], T["q1x"].at[plane[j], b, c], at(a0, b0, c))
                    part[blk, lo] = value[:lo.size].astype(BF16)
                    part[blk, hi] = edge.astype(BF16)
                start([out(blk, 0, None, ry.at[plane[j], b0], T["qy"].at[plane[j], b0], at(a0, b, c0))])

        def column_sum(j):
            value = product(at(plane[j], b0, c0))
            for c in xs:
                value = value + landed(rx.at[plane[j], c], T["qx"].at[plane[j], c], at(a0, b0, c))
            for b in ys:
                value = value + landed(ry.at[plane[j], b], T["qy"].at[plane[j], b], at(a0, b, c0))
            return value

        def reduce0():
            for j in range(2, A):
                for b, c in cells:
                    blk = at(plane[j], b, c)
                    part[blk] = product(blk).astype(BF16)
                    split(blk, j, b, c)
            for b, c in cells:
                blk = at(plane[1], b, c)
                part[blk] = product(blk).astype(BF16)
                start([out(blk, 0, None, rd.at[b, c], T["qd"].at[b, c], at(plane[1], b0, c0))])

        def reduce1():
            side_sums(1)
            for j in range(2, A):
                side_sums(j)
            for b, c in cells:
                blk = at(a0, b, c)
                value = product(blk) + landed(rd.at[b, c], T["qd"].at[b, c], at(plane[1], b0, c0))
                part[blk] = value.astype(BF16)
                split(blk, 0, b, c)

        def reduce2():
            for j in range(1, A):
                blk = at(plane[j], b0, c0)
                part[blk] = column_sum(j).astype(BF16)
                start([out(blk, 0, None, rz.at[a0], T["qz"].at[a0], at(plane[j], b0, c0))])
            side_sums(0)

        def gradient():
            share = column_sum(0)
            for j in range(1, A):
                share = share + landed(rz.at[plane[j]], T["qz"].at[plane[j]], at(plane[j], b0, c0))
            proj = to_column(stat_sum(0, T["st_pr"]), 128)
            inv = T["inv"][:, 0:1]
            scaled = unpack(share, rp, dl) * gain3[me]
            cot = pad_rows(cot_in[r0:r0 + real].astype(F32), rp)
            grad = cot + inv * scaled - own_x() * (inv * inv * (proj[:, 0:1] / width))
            T["gg"][me] = pack(grad).astype(BF16)

        def score(blocks):
            for blk in blocks:
                value = unpack(T["gg"][blk].astype(F32), rp, dl).astype(BF16)
                T["scores"][...] += lax.dot_general(value, emb3[blk], NT, preferred_element_type=F32)

        def member_copy(d):
            return remote(T["scores"], T["others"].at[mine], T["m_send"].at[d], T["m_recv"].at[mine],
                          turn(mine, d, members), "member")

        def exchange():
            start([member_copy(d) for d in range(1, members)])

        def current():
            total = T["scores"][...]
            for d in range(1, members):
                src = turn(mine, d, members)
                slot = T["others"].at[src]
                remote(slot, slot, T["m_send"].at[d], T["m_recv"].at[src], src, "member").wait_recv()
                total = total + slot[...]
            T["total"][...] = total
            entry = (lax.broadcasted_iota(jnp.int32, (rp, vl), 1) + me * vl).astype(F32)
            st_in[1] = to_row(jnp.where(idcol[r0:r0 + rp, 0:1] == entry, total, 0.0))
            stat_send(1, T["st_cu"])

        def finish():
            column = to_column(stat_sum(1, T["st_cu"]), 128)
            out_ref[r0:r0 + real] = (T["total"][...] - column[:, 0:1])[0:real]

        x_stages = gather(T["xg"], T["x_send"], T["x_recv"], up)
        g_stages = gather(T["gg"], T["g_send"], T["g_recv"], score)
        def own_pack():
            T["xg"][me] = pack(own_x()).astype(BF16)

        def clear():
            T["acc"][...] = jnp.zeros_like(T["acc"])
            T["ssq"][...] = jnp.zeros_like(T["ssq"])
            T["scores"][...] = jnp.zeros_like(T["scores"])

        def turn_around():
            gradient()
            g_stages[0]()

        def seq(*stages):
            def stage():
                for part_ in stages:
                    part_()
            return stage

        timed = x_stages[1:3] + [seq(x_stages[3], activate, reduce0), reduce1, reduce2, turn_around]
        timed += g_stages[1:3] + [seq(g_stages[3], exchange), current, finish]
        return own_pack, clear, x_stages[0], timed

    plans = [program(k) for k in range(len(chunks))]
    for own_pack, _, _, _ in plans:
        own_pack()
    pl.semaphore_wait(barrier, n - 1 + members - 1)
    for _, _, begin, _ in plans:
        begin()
    for _, clear, _, _ in plans:
        clear()
    for b in range(n):
        gain3[b] = gain_in[:, b * dl:(b + 1) * dl]
    loads[0].wait()
    loads[1].wait()
    for b in range(n):
        wt3[b, 0:fl] = S["wg_v"][:, b * dl:(b + 1) * dl]
        wt3[b, flp:flp + fl] = S["wu_v"][:, b * dl:(b + 1) * dl]
        if flp > fl:
            wt3[b, fl:flp] = jnp.zeros((flp - fl, dl), BF16)
            wt3[b, flp + fl:] = jnp.zeros((flp - fl, dl), BF16)
    loads[2].wait()
    for b in range(n):
        emb3[b] = S["emb_v"][:, b * dl:(b + 1) * dl]
    ids = to_column(ids_in[...].astype(F32), 128)
    idcol[...] = pad_rows(ids, idcol.shape[0])

    timeline = []
    for k, (_, _, _, timed) in enumerate(plans):
        timeline += [(i + LAG * k, k, stage) for i, stage in enumerate(timed)]
    for _, _, stage in sorted(timeline, key=lambda item: item[:2]):
        stage()
    for copy in waits:
        copy.wait_send()


def split_rows(rows):
    size = ceil_to(-(-rows // PARTS), 16)
    return [(r, min(size, rows - r), ceil_to(min(size, rows - r), 8)) for r in range(0, rows, size)]


def on_device(n, members, layer_input, norm_gain, w_gate, w_up, hidden_cot, output_cot, embed, suffix_ids):
    _, rows, dl = layer_input.shape
    width = norm_gain.shape[1]
    fl = w_gate.shape[2]
    vl = embed.shape[1]
    lines = A, B, C = grid_of(n)
    chunks = split_rows(rows)
    flp = ceil_to(fl, 128)
    sends = gather_sends(lines)
    vmem = pl.BlockSpec(memory_space=pltpu.VMEM)
    hbm = pl.BlockSpec(memory_space=pl.ANY)
    dma = pltpu.SemaphoreType.DMA
    V = pltpu.VMEM
    scratch = [
        V((fl, width), BF16), V((fl, width), BF16), V((n, 2 * flp, dl), BF16),
        V((vl, width), BF16), V((n, vl, dl), BF16), V((n, 1, dl), F32),
        V((chunks[-1][0] + chunks[-1][2], 128), F32), dma((3,)),
    ]
    for _, _, rp in chunks:
        length = packed_rows(rp, dl)
        block = (length, 128)
        scratch += [
            V((n, *block), BF16), V((n, *block), BF16), V((n, *block), BF16),
            V((A, C, *block), BF16), V((A, B, *block), BF16), V((A, *block), BF16), V((B, C, *block), BF16),
            V((A, C, B, *block), BF16), V((A, B, C, *block), BF16),
            V((2, 1, rp), F32), V((n, 1, rp), F32), V((n, 1, rp), F32),
            V((rp, 2 * flp), F32), V((rp, 2 * flp), BF16), V((rp, 128), F32), V(block, F32),
            V((rp, vl), F32), V((members, rp, vl), F32), V((rp, vl), F32),
            dma((sends,)), dma((n, 2)), dma((sends,)), dma((n, 2)), dma((n, 2)),
            dma((A, C)), dma((A, B)), dma((A,)), dma((B, C)), dma((A, C, B)), dma((A, B, C)),
            dma((2, n)), dma((2, n)), dma((members,)), dma((members,)),
        ]
    return pl.pallas_call(
        functools.partial(kernel, n, members, lines, chunks, width),
        out_shape=jax.ShapeDtypeStruct((rows, vl), F32),
        in_specs=[vmem] * 5 + [hbm] * 3,
        out_specs=vmem,
        scratch_shapes=scratch,
        compiler_params=pltpu.CompilerParams(
            collective_id=0, has_side_effects=True, vmem_limit_bytes=60 * 1024 * 1024
        ),
    )(layer_input[0], norm_gain, hidden_cot[0], output_cot[0], suffix_ids[None, :],
      w_gate[0].T, w_up[0].T, embed[0])


def solution(mesh):
    n, members = mesh.shape["shard"], mesh.shape["member"]
    placed = (
        P("member", None, "shard"),
        P("member", None),
        P("member", None, "shard"),
        P("member", None, "shard"),
        P("member", None, "shard"),
        P("member", None, "shard"),
        P("member", "shard", None),
        P(),
    )
    return jax.shard_map(
        functools.partial(on_device, n, members),
        mesh=mesh, in_specs=placed, out_specs=P(None, "shard"), check_vma=False,
    )
```
